128 devices in a mesh: req: 16 (over y, z), tp: 8 (over x, core).
Axes of the slice: x: 4, y: 4, z: 4, core: 2. Of those that a mesh axis runs over, the one named last changes fastest.
Arguments:
- short_tokens: bfloat16 [1536, 3072], P('req')
- long_tokens: bfloat16 [8, 3072], replicated
- norm_gain: bfloat16 [3072], replicated, may hold values from 0.5 to 1.5
- w_query: bfloat16 [3072, 3072], P(None, 'tp'), may hold values from -0.109375 to 0.109375
- w_key: bfloat16 [3072, 1024], P(None, 'tp'), may hold values from -0.109375 to 0.109375
- w_value: bfloat16 [3072, 1024], P(None, 'tp'), may hold values from -0.109375 to 0.109375
- w_out: bfloat16 [3072, 3072], P('tp'), may hold values from -0.109375 to 0.109375
- short_lengths: int32 [1536], P('req'), may hold values from 0 to 127
- long_lengths: int32 [8], replicated, may hold values from 6144 to 8191
- short_cache: bfloat16 [1536, 8, 128, 256], P('req', 'tp'), may hold values from -120 to 120
- long_cache: bfloat16 [8, 8, 8192, 256], P(None, 'tp', 'req'), may hold values from -120 to 120
Outputs:
- short_hidden: bfloat16 [1536, 3072], P('req')
- long_hidden: bfloat16 [8, 3072], replicated
- short_cache_new: bfloat16 [1536, 8, 128, 256], P('req', 'tp')
- long_cache_new: bfloat16 [8, 8, 8192, 256], P(None, 'tp', 'req')
The draws below stay inside these ranges and needn't reach their ends.
All inputs are finite; a program needn't handle non-finite values.
Results may differ from the reference program's by a relative error of at most 0.0095.
Values may be sent and summed in bfloat16 or wider, within the bound.
A program may use at most 128 MiB of HBM per device.

```python
import jax
import jax.numpy as jnp
from jax import lax

D = 3072
QH = 24
KVH = 8
HD = 128
SCAP = 128
LONGS = 8
LCAP = 8192
REQS = 1536
GROUP = 3


def token_law(key, count):
    key_base = jax.random.fold_in(key, 0)
    base = jnp.clip(jax.random.normal(key_base, (count, D), jnp.float32), -6.0, 6.0)
    return base.astype(jnp.bfloat16)


def cache_law(key, leading, slots, block):
    key_keys = jax.random.fold_in(key, 0)
    key_vals = jax.random.fold_in(key, 2)
    key_offs = jax.random.fold_in(key, 3)
    key_part = jnp.clip(jax.random.normal(key_keys, (leading, KVH, slots, HD), jnp.float32), -6.0, 6.0)
    noise = jnp.clip(jax.random.normal(key_vals, (leading, KVH, slots // block, block, HD), jnp.float32), -6.0, 6.0)
    offsets = 3.0 * jnp.clip(jax.random.normal(key_offs, (leading, KVH, slots // block, 1, HD), jnp.float32), -6.0, 6.0)
    value_part = (noise + offsets).reshape(leading, KVH, slots, HD)
    return jnp.concatenate([key_part, value_part], axis=-1).astype(jnp.bfloat16)


def draw_short_tokens(key, part):
    return token_law(jax.random.fold_in(key, 11), REQS)


def draw_long_tokens(key, part):
    return token_law(jax.random.fold_in(key, 12), LONGS)


def draw_short_cache(key, part):
    return cache_law(jax.random.fold_in(key, 21), REQS, SCAP, 8)


def draw_long_cache(key, part):
    return cache_law(jax.random.fold_in(key, 22), LONGS, LCAP, 32)


def draw_short_lengths(key, part):
    key_first, key_second, key_spots = jax.random.split(jax.random.fold_in(key, 31), 3)
    first = jax.random.randint(key_first, (REQS,), 0, SCAP)
    second = jax.random.randint(key_second, (REQS,), 0, SCAP)
    lengths = first * second // (SCAP - 1)
    spots = jax.random.permutation(key_spots, REQS)
    lengths = lengths.at[spots[0]].set(SCAP - 1).at[spots[1]].set(0)
    return lengths.astype(jnp.int32)


def draw_long_lengths(key, part):
    key_vals, key_spots = jax.random.split(jax.random.fold_in(key, 41), 2)
    lowest = LCAP * 3 // 4
    lengths = jax.random.randint(key_vals, (LONGS,), lowest, LCAP)
    spots = jax.random.permutation(key_spots, LONGS)
    lengths = lengths.at[spots[0]].set(LCAP - 1).at[spots[1]].set(lowest)
    return lengths.astype(jnp.int32)


def level_of(key, extent, pieces, least, top_value):
    def one(position, blocks):
        heights = jax.random.uniform(jax.random.fold_in(jax.random.fold_in(key, 6), position), (blocks,), jnp.float32, least / len(pieces), top_value / len(pieces))
        return jnp.repeat(jnp.exp(heights), extent[position] // blocks).reshape((-1,) + (1,) * (len(extent) - position - 1))

    level = one(*pieces[0])
    for cut in pieces[1:]:
        level = level * one(*cut)
    return level


def normal_values(key, extent, width, bound, pieces=(), held_as=jnp.bfloat16):
    loudness = level_of(key, extent, pieces, -0.22, 0.18) if pieces else 1.0
    values = jax.random.normal(key, extent, jnp.float32) * width * loudness
    return jnp.minimum(jnp.maximum(values, -bound), bound).astype(held_as)


def setup_inputs(seed: int = 0) -> dict:
    key_of = jax.random.split(jax.random.key(seed), 12)
    short_tokens = draw_short_tokens(jax.random.fold_in(key_of[11], 71), 0)
    long_tokens = draw_long_tokens(jax.random.fold_in(key_of[11], 71), 0)
    norm_gain = jnp.clip(jax.random.uniform(key_of[2], (D,), jnp.float32, 0.5, 1.5), 0.5, 1.5).astype(jnp.bfloat16)
    w_query = normal_values(key_of[3], (D, QH * HD), D ** -0.5, 0.109375, ((1, 8),))
    w_key = normal_values(key_of[4], (D, KVH * HD), D ** -0.5, 0.109375, ((1, 8),))
    w_value = normal_values(key_of[5], (D, KVH * HD), D ** -0.5, 0.109375, ((1, 8),))
    w_out = normal_values(key_of[6], (QH * HD, D), (QH * HD) ** -0.5, 0.109375, ((0, 8),))
    short_lengths = draw_short_lengths(jax.random.fold_in(key_of[11], 71), 0)
    long_lengths = draw_long_lengths(jax.random.fold_in(key_of[11], 71), 0)
    short_cache = draw_short_cache(jax.random.fold_in(key_of[11], 71), 0)
    long_cache = draw_long_cache(jax.random.fold_in(key_of[11], 71), 0)
    return {"short_tokens": short_tokens, "long_tokens": long_tokens, "norm_gain": norm_gain, "w_query": w_query, "w_key": w_key, "w_value": w_value, "w_out": w_out, "short_lengths": short_lengths, "long_lengths": long_lengths, "short_cache": short_cache, "long_cache": long_cache}


rope_theta = 500000.0
floor_score = -1e+30

def rotate(values, positions):
    half = values.shape[-1] // 2
    freq = rope_theta ** (-(jnp.arange(half, dtype=jnp.float32) * 2.0 / values.shape[-1]))
    angle = positions.astype(jnp.float32)[:, None] * freq[None, :]
    cosine = jnp.cos(angle)[:, None, :]
    sine = jnp.sin(angle)[:, None, :]
    front = values[..., :half]
    back = values[..., half:]
    return jnp.concatenate([front * cosine - back * sine, back * cosine + front * sine], axis=-1)

def attend(query_head, cache_head, lengths, round_weights):
    key_part = cache_head[..., :HD].astype(jnp.float32)
    value_part = cache_head[..., HD:].astype(jnp.float32)
    scores = jnp.einsum('bgd,bsd->bgs', query_head.astype(jnp.float32), key_part, precision=lax.Precision.HIGHEST) / jnp.sqrt(jnp.float32(HD))
    slot_ids = jnp.arange(cache_head.shape[1], dtype=jnp.int32)
    is_valid = slot_ids[None, None, :] <= lengths[:, None, None]
    scores = jnp.where(is_valid, scores, floor_score)
    top = lax.optimization_barrier(jnp.max(scores, axis=-1, keepdims=True))
    expo = jnp.where(is_valid, jnp.exp(scores - top), 0.0)
    weights = expo / lax.optimization_barrier(jnp.sum(expo, axis=-1, keepdims=True))
    if round_weights:
        weights = lax.optimization_barrier(weights.astype(jnp.bfloat16)).astype(jnp.float32)
    return jnp.einsum('bgs,bsd->bgd', weights, value_part, precision=lax.Precision.HIGHEST)

def reference(short_tokens, long_tokens, norm_gain, w_query, w_key, w_value, w_out, short_lengths, long_lengths, short_cache, long_cache):
    all_tokens = jnp.concatenate([short_tokens, long_tokens], axis=0)
    positions = jnp.concatenate([short_lengths, long_lengths], axis=0)
    wide = all_tokens.astype(jnp.float32)
    normed = (wide * lax.rsqrt(lax.optimization_barrier(jnp.mean(wide * wide, axis=-1, keepdims=True)) + 1e-05) * norm_gain.astype(jnp.float32)).astype(jnp.bfloat16)
    total_rows = all_tokens.shape[0]
    query = jnp.dot(normed, w_query, preferred_element_type=jnp.float32).reshape(total_rows, QH, HD)
    query = rotate(query, positions).astype(jnp.bfloat16).reshape(total_rows, KVH, GROUP, HD)
    key_new = jnp.dot(normed, w_key, preferred_element_type=jnp.float32).reshape(total_rows, KVH, HD)
    key_new = rotate(key_new, positions).astype(jnp.bfloat16)
    value_new = jnp.dot(normed, w_value, preferred_element_type=jnp.float32).reshape(total_rows, KVH, HD).astype(jnp.bfloat16)
    fresh = jnp.concatenate([key_new, value_new], axis=-1)
    short_slots = jnp.arange(SCAP, dtype=jnp.int32)
    short_write = short_slots[None, :] == short_lengths[:, None]
    short_cache_new = jnp.where(short_write[:, None, :, None], fresh[:REQS, :, None, :], short_cache)
    long_slots = jnp.arange(LCAP, dtype=jnp.int32)
    long_write = long_slots[None, :] == long_lengths[:, None]
    long_cache_new = jnp.where(long_write[:, None, :, None], fresh[REQS:, :, None, :], long_cache)

    def short_head(index):
        cache_head = lax.dynamic_index_in_dim(short_cache_new, index, 1, keepdims=False)
        query_head = lax.dynamic_index_in_dim(query[:REQS], index, 1, keepdims=False)
        return attend(query_head, cache_head, short_lengths, True)

    def long_head(index):
        cache_head = lax.dynamic_index_in_dim(long_cache_new, index, 1, keepdims=False)
        query_head = lax.dynamic_index_in_dim(query[REQS:], index, 1, keepdims=False)
        return attend(query_head, cache_head, long_lengths, False)
    head_ids = jnp.arange(KVH, dtype=jnp.int32)
    short_mix = jnp.transpose(lax.map(short_head, head_ids), (1, 0, 2, 3)).reshape(REQS, QH * HD)
    long_mix = jnp.transpose(lax.map(long_head, head_ids), (1, 0, 2, 3)).reshape(LONGS, QH * HD)
    mixed = jnp.concatenate([short_mix, long_mix], axis=0).astype(jnp.bfloat16)
    head_out = jnp.dot(mixed, w_out, preferred_element_type=jnp.float32)
    hidden = (wide + head_out).astype(jnp.bfloat16)
    return (hidden[:REQS], hidden[REQS:], short_cache_new, long_cache_new)
```

```python
import functools
import math

import jax
import jax.numpy as jnp
import numpy as np
from jax import lax
from jax.experimental import pallas as pl
from jax.experimental.pallas import tpu as pltpu
from jax.sharding import PartitionSpec as P

rope_theta = 500000.0
floor_score = -1e30
group_rows = 16
MESH = pl.DeviceIdType.MESH
F32 = jnp.float32
BF16 = jnp.bfloat16


def nt_dot(a, b):
    return lax.dot_general(a, b, (((1,), (1,)), ((), ())), preferred_element_type=F32)


def attend_kernel(
    short_len,
    long_len,
    tokens,
    long_tokens,
    gain,
    freq,
    w_query,
    w_key,
    w_value,
    short_cache,
    long_cache,
    att_out,
    part_out,
    short_new,
    long_new,
    tok_v,
    ltok_v,
    normed,
    wq_v,
    wk_v,
    wv_v,
    pos_v,
    q_v,
    qlong_v,
    fresh_v,
    cache_v,
    long_v,
    tok_sem,
    w_sem,
    in_sem,
    out_sem,
    lin_sem,
    lout_sem,
):
    short_count = tokens.shape[0]
    long_count = long_tokens.shape[0]
    slots = short_cache.shape[1]
    span = long_cache.shape[1]
    head = short_cache.shape[2] // 2
    heads = w_query.shape[1] // head
    groups = short_count // group_rows
    rows = heads * group_rows
    lrows = heads * long_count
    scale = 1.0 / math.sqrt(head)

    def cache_in(g):
        view = pl.ds(g * group_rows, group_rows)
        return pltpu.make_async_copy(short_cache.at[view], cache_v.at[view], in_sem.at[g])

    def cache_out(g):
        view = pl.ds(g * group_rows, group_rows)
        return pltpu.make_async_copy(cache_v.at[view], short_new.at[view], out_sem.at[g])

    first = [
        pltpu.make_async_copy(tokens, tok_v, tok_sem.at[0]),
        pltpu.make_async_copy(long_tokens, ltok_v, tok_sem.at[1]),
    ]
    weights = [
        pltpu.make_async_copy(w_key, wk_v, w_sem.at[0]),
        pltpu.make_async_copy(w_value, wv_v, w_sem.at[1]),
        pltpu.make_async_copy(w_query, wq_v, w_sem.at[2]),
    ]
    long_in = pltpu.make_async_copy(long_cache, long_v, lin_sem)
    long_out = pltpu.make_async_copy(long_v, long_new, lout_sem)
    for copy in first + weights:
        copy.start()
    long_in.start()
    for g in range(groups):
        cache_in(g).start()

    sub8 = lax.broadcasted_iota(jnp.int32, (8, head), 0)
    for tile in range((short_count + long_count) // 8):
        value = jnp.zeros((8, head), jnp.int32)
        for j in range(8):
            r = tile * 8 + j
            length = short_len[r] if r < short_count else long_len[r - short_count]
            value = jnp.where(sub8 == j, length, value)
        pos_v[tile * 8 : tile * 8 + 8, :] = value

    gain_row = gain[...].astype(F32)

    def norm_rows(value):
        value = value.astype(F32)
        mean = jnp.mean(value * value, axis=-1, keepdims=True)
        return (value * lax.rsqrt(mean + 1e-05) * gain_row).astype(BF16)

    for copy in first:
        copy.wait()

    def norm_step(i, carry):
        view = pl.ds(pl.multiple_of(i * 16, 16), 16)
        normed[view, :] = norm_rows(tok_v[view, :])
        return carry

    lax.fori_loop(0, short_count // 16, norm_step, 0)
    tail = jnp.concatenate([ltok_v[...].astype(F32), jnp.zeros((16 - long_count, tok_v.shape[1]), F32)], axis=0)
    normed[short_count : short_count + 16, :] = norm_rows(tail)

    total_rows = short_count + long_count
    angle = pos_v[...].astype(F32) * freq[...]
    cosine = jnp.cos(angle)
    lane = lax.broadcasted_iota(jnp.int32, angle.shape, 1)
    sine = jnp.where(lane < head // 2, -jnp.sin(angle), jnp.sin(angle))

    def rotate(value):
        return value * cosine + pltpu.roll(value, head // 2, 1) * sine

    weights[0].wait()
    key = jnp.dot(normed[...], wk_v[...], preferred_element_type=F32)[:total_rows]
    fresh_v[:, :head] = rotate(key).astype(BF16).astype(F32)
    weights[1].wait()
    value = jnp.dot(normed[...], wv_v[...], preferred_element_type=F32)[:total_rows]
    fresh_v[:, head:] = value.astype(BF16).astype(F32)
    weights[2].wait()
    query = jnp.dot(normed[...], wq_v[...], preferred_element_type=F32)[:total_rows]
    for h in range(heads):
        rotated = rotate(query[:, h * head : (h + 1) * head])
        q_v[:, h * head : (h + 1) * head] = rotated[:short_count].astype(BF16)
        qlong_v[h * long_count : (h + 1) * long_count, :] = rotated[short_count:]

    sub16 = lax.broadcasted_iota(jnp.int32, (16, 2 * head), 0)

    def patch(ref, slot, limit, row):
        start = pl.multiple_of(lax.clamp(0, slot // 16, limit // 16 - 1) * 16, 16)
        old = ref[pl.ds(start, 16), :].astype(F32)
        new = fresh_v[pl.ds(row, 1), :]
        ref[pl.ds(start, 16), :] = jnp.where(sub16 + start == slot, new, old).astype(BF16)

    first_slot = lax.axis_index("req") * span
    long_in.wait()
    for l in range(long_count):
        patch(long_v.at[l], long_len[l] - first_slot, span, short_count + l)
    qlong = qlong_v[...].astype(BF16)
    row_of = lax.rem(lax.broadcasted_iota(jnp.int32, (lrows, span), 0), long_count)
    slot_of = lax.broadcasted_iota(jnp.int32, (lrows, span), 1) + first_slot
    long_pos = jnp.concatenate([pos_v[short_count:total_rows, :]] * heads, axis=0)
    long_pos = jnp.concatenate([long_pos] * (span // head), axis=1)
    long_valid = slot_of <= long_pos
    scores = jnp.full((lrows, span), floor_score, F32)
    for l in range(long_count):
        piece = nt_dot(qlong, long_v[l, :, :head])
        scores = jnp.where(row_of == l, piece, scores)
    scores = jnp.where(long_valid, scores * scale, floor_score)
    peak = jnp.max(scores, axis=-1, keepdims=True)
    expo = jnp.where(long_valid, jnp.exp(scores - peak), 0.0)
    total = jnp.sum(expo, axis=-1, keepdims=True)
    summed = jnp.zeros((lrows, head), F32)
    for l in range(long_count):
        weight = jnp.where(row_of == l, expo, 0.0).astype(BF16)
        summed = summed + jnp.dot(weight, long_v[l, :, head:], preferred_element_type=F32)
    part_out[:lrows, :] = summed
    here = lax.broadcasted_iota(jnp.int32, (lrows, head), 0) == lax.broadcasted_iota(
        jnp.int32, (lrows, head), 1
    )
    peak_row = jnp.sum(jnp.where(here, peak, 0.0), axis=0, keepdims=True)
    total_row = jnp.sum(jnp.where(here, total, 0.0), axis=0, keepdims=True)
    part_out[lrows : lrows + 8, :] = jnp.where(sub8 == 0, peak_row, total_row)
    long_out.start()

    row16 = lax.rem(lax.broadcasted_iota(jnp.int32, (rows, head), 0), group_rows)
    lane16 = lax.broadcasted_iota(jnp.int32, (rows, head), 1)

    def group(g, carry):
        cache_in(g).wait()
        base = pl.multiple_of(g * group_rows, group_rows)
        for j in range(group_rows):
            patch(cache_v.at[base + j], short_len[base + j], slots, base + j)
        block = q_v[pl.ds(base, group_rows), :]
        stacked = jnp.concatenate([block[:, h * head : (h + 1) * head] for h in range(heads)], axis=0)
        score = jnp.full((rows, slots), floor_score, F32)
        for j in range(group_rows):
            piece = nt_dot(stacked, cache_v[base + j, :, :head])
            score = jnp.where(row16 == j, piece, score)
        valid = lane16 <= jnp.concatenate([pos_v[pl.ds(base, group_rows), :]] * heads, axis=0)
        score = jnp.where(valid, score * scale, floor_score)
        top = jnp.max(score, axis=-1, keepdims=True)
        expo_s = jnp.where(valid, jnp.exp(score - top), 0.0)
        weight = expo_s / jnp.sum(expo_s, axis=-1, keepdims=True)
        mix = jnp.zeros((rows, head), F32)
        for j in range(0, group_rows, 2):
            pair = jnp.concatenate(
                [jnp.where(row16 == i, weight, 0.0).astype(BF16) for i in (j, j + 1)], axis=1
            )
            values = cache_v[pl.ds(base + j, 2), :, head:].reshape(2 * slots, head)
            mix = mix + jnp.dot(pair, values, preferred_element_type=F32)
        att_out[pl.ds(base, group_rows), :] = jnp.concatenate(
            [mix[h * group_rows : (h + 1) * group_rows] for h in range(heads)], axis=1
        ).astype(BF16)
        cache_out(g).start()
        return carry

    lax.fori_loop(0, groups, group, 0)
    for g in range(groups):
        cache_out(g).wait()
    long_out.wait()


def merge_parts(parts, lrows, head):
    here = lax.broadcasted_iota(jnp.int32, (lrows, head), 0) == lax.broadcasted_iota(
        jnp.int32, (lrows, head), 1
    )
    peaks = [part[lrows : lrows + 1, :] for part in parts]
    totals = [part[lrows + 1 : lrows + 2, :] for part in parts]
    top = functools.reduce(jnp.maximum, peaks)
    total = jnp.zeros_like(top)
    summed = jnp.zeros((lrows, head), F32)
    for part, peak, some in zip(parts, peaks, totals):
        factor = jnp.exp(peak - top)
        total = total + some * factor
        column = jnp.sum(jnp.where(here, factor, 0.0), axis=1, keepdims=True)
        summed = summed + part[:lrows, :] * column
    return top, total, summed


def project_kernel(
    tp_size,
    grid_size,
    att,
    part,
    w_out,
    tokens,
    long_tokens,
    hidden,
    long_hidden,
    w_v,
    res_v,
    lres_v,
    part_y,
    part_z,
    mine_v,
    pair_send,
    pair_recv,
    own_v,
    chip_send,
    chip_recv,
    hid_v,
    lsend_v,
    lrecv_v,
    lhid_v,
    w_sem,
    res_sem,
    y_send,
    y_recv,
    z_send,
    z_recv,
    ps_sem,
    pr_sem,
    cs_sem,
    cr_sem,
    gs_sem,
    gr_sem,
    fs_sem,
    fr_sem,
    ls_sem,
    lr_sem,
    lgs_sem,
    lgr_sem,
    out_sem,
    lout_sem,
):
    req = lax.axis_index("req")
    me = lax.axis_index("tp")
    chips = tp_size // 2
    core = lax.rem(me, 2)
    chip = me // 2
    row = req // grid_size
    col = lax.rem(req, grid_size)
    lrows = part.shape[0] - 8
    head = part.shape[1]
    long_count = long_tokens.shape[0]
    heads = lrows // long_count
    width = w_out.shape[1] // tp_size

    def at_tp(index):
        return (req, index)

    partner = chip * 2 + 1 - core
    peers = [lax.rem(me + d, tp_size) for d in range(1, tp_size)]
    row_peers = [(lax.rem(row + d, grid_size) * grid_size + col, me) for d in range(1, grid_size)]
    col_peers = [(row * grid_size + lax.rem(col + d, grid_size), me) for d in range(1, grid_size)]
    chip_peers = [lax.rem(chip + d, chips) for d in range(chips)]

    barrier = pltpu.get_barrier_semaphore()
    everyone = [at_tp(index) for index in peers] + row_peers + col_peers
    for device in everyone:
        pl.semaphore_signal(barrier, inc=1, device_id=device, device_id_type=MESH)

    def columns(j):
        return pl.ds(pl.multiple_of(j * width, width), width)

    w_copies = []
    for j in range(tp_size):
        w_copies.append(pltpu.make_async_copy(w_out.at[:, columns(j)], w_v.at[j], w_sem.at[j]))
        w_copies[-1].start()
    res_copy = pltpu.make_async_copy(tokens.at[:, columns(me)], res_v, res_sem.at[0])
    lres_copy = pltpu.make_async_copy(long_tokens.at[:, columns(me)], lres_v, res_sem.at[1])
    res_copy.start()
    lres_copy.start()
    pl.semaphore_wait(barrier, len(everyone))

    def remote(src, dst, send, recv, device):
        return pltpu.make_async_remote_copy(
            src_ref=src, dst_ref=dst, send_sem=send, recv_sem=recv, device_id=device, device_id_type=MESH
        )

    y_copies = [
        remote(part, part_y.at[d], y_send.at[d], y_recv.at[d], device) for d, device in enumerate(row_peers)
    ]
    for copy in y_copies:
        copy.start()
    for copy in w_copies:
        copy.wait()

    order = [chips // 2] + [d for d in range(1, chips) if d != chips // 2] + [0]
    pair_copies = []
    for d in order:
        j = chip_peers[d] * 2 + 1 - core
        pair_send[d] = jnp.dot(att[...], w_v[j], preferred_element_type=F32).astype(BF16)
        copy = remote(pair_send.at[d], pair_recv.at[d], ps_sem.at[d], pr_sem.at[d], at_tp(partner))
        copy.start()
        pair_copies.append(copy)
    for d in range(chips):
        j = chip_peers[d] * 2 + core
        own_v[d] = jnp.dot(att[...], w_v[j], preferred_element_type=F32)
    chip_copies = []
    for place, d in enumerate(order):
        pair_copies[place].wait_recv()
        summed = own_v[d] + pair_recv[d].astype(F32)
        if d == 0:
            own_v[d] = summed
        else:
            chip_send[d - 1] = summed.astype(BF16)
            copy = remote(
                chip_send.at[d - 1],
                chip_recv.at[d - 1],
                cs_sem.at[d - 1],
                cr_sem.at[d - 1],
                at_tp(chip_peers[d] * 2 + core),
            )
            copy.start()
            chip_copies.append(copy)

    sub8 = lax.broadcasted_iota(jnp.int32, (8, head), 0)
    for copy in y_copies:
        copy.wait_recv()
    top, total, summed = merge_parts([part[...]] + [part_y[d] for d in range(grid_size - 1)], lrows, head)
    mine_v[:lrows, :] = summed
    mine_v[lrows:, :] = jnp.where(sub8 == 0, top, total)
    z_copies = [
        remote(mine_v, part_z.at[d], z_send.at[d], z_recv.at[d], device) for d, device in enumerate(col_peers)
    ]
    for copy in z_copies:
        copy.start()
    for copy in z_copies:
        copy.wait_recv()
    top, total, summed = merge_parts([mine_v[...]] + [part_z[d] for d in range(grid_size - 1)], lrows, head)
    here = lax.broadcasted_iota(jnp.int32, (lrows, head), 0) == lax.broadcasted_iota(
        jnp.int32, (lrows, head), 1
    )
    mixed = summed / jnp.sum(jnp.where(here, total, 0.0), axis=1, keepdims=True)
    long_att = jnp.concatenate(
        [mixed[h * long_count : (h + 1) * long_count] for h in range(heads)], axis=1
    ).astype(BF16)
    long_copies = []
    for d in range(tp_size):
        j = lax.rem(me + d, tp_size)
        lsend_v[d] = jnp.dot(long_att, w_v[j], preferred_element_type=F32)
        if d:
            copy = remote(
                lsend_v.at[d], lrecv_v.at[d - 1], ls_sem.at[d - 1], lr_sem.at[d - 1], at_tp(peers[d - 1])
            )
            copy.start()
            long_copies.append(copy)

    res_copy.wait()
    lres_copy.wait()
    acc = own_v[0] + res_v[...].astype(F32)
    for d in range(1, chips):
        chip_copies[order.index(d)].wait_recv()
        acc = acc + chip_recv[d - 1].astype(F32)
    hid_v[me] = acc.astype(BF16)
    gather = []
    for d in range(1, chips):
        copy = remote(
            hid_v.at[me], hid_v.at[me], gs_sem.at[d - 1], gr_sem.at[d - 1], at_tp(chip_peers[d] * 2 + core)
        )
        copy.start()
        gather.append(copy)
    forward = [remote(hid_v.at[me], hid_v.at[me], fs_sem.at[0], fr_sem.at[0], at_tp(partner))]
    forward[0].start()
    outs = []

    def put(j):
        copy = pltpu.make_async_copy(hid_v.at[j], hidden.at[:, columns(j)], out_sem.at[len(outs)])
        copy.start()
        outs.append(copy)

    put(me)

    for copy in long_copies:
        copy.wait_recv()
    lacc = lsend_v[0] + lres_v[...].astype(F32)
    for d in range(tp_size - 1):
        lacc = lacc + lrecv_v[d]
    lhid_v[me] = lacc.astype(BF16)
    long_gather = []
    for d in range(tp_size - 1):
        copy = remote(lhid_v.at[me], lhid_v.at[me], lgs_sem.at[d], lgr_sem.at[d], at_tp(peers[d]))
        copy.start()
        long_gather.append(copy)

    for d in range(1, chips):
        source = lax.rem(chip + chips - d, chips) * 2 + core
        gather[d - 1].wait_recv()
        copy = remote(hid_v.at[source], hid_v.at[source], fs_sem.at[d], fr_sem.at[d], at_tp(partner))
        copy.start()
        forward.append(copy)
        put(source)
    for d in range(chips):
        forward[d].wait_recv()
        put(lax.rem(chip + chips - d, chips) * 2 + 1 - core)
    for copy in long_gather:
        copy.wait_recv()
    louts = []
    for j in range(tp_size):
        copy = pltpu.make_async_copy(lhid_v.at[j], long_hidden.at[:, columns(j)], lout_sem.at[j])
        copy.start()
        louts.append(copy)
    for copy in y_copies + pair_copies + chip_copies + z_copies + long_copies + gather + forward + long_gather:
        copy.wait_send()
    for copy in outs + louts:
        copy.wait()


def per_device(
    tp_size,
    req_size,
    short_tokens,
    long_tokens,
    norm_gain,
    w_query,
    w_key,
    w_value,
    w_out,
    short_lengths,
    long_lengths,
    short_cache,
    long_cache,
):
    short_count, model = short_tokens.shape
    long_count = long_tokens.shape[0]
    slots, head = short_cache.shape[2], short_cache.shape[3] // 2
    span = long_cache.shape[2]
    query_width = w_query.shape[1]
    heads = query_width // head
    total_rows = short_count + long_count
    lrows = heads * long_count
    groups = short_count // group_rows
    half = rope_theta ** (-(np.arange(head // 2, dtype=np.float64) * 2.0 / head))
    freq = np.concatenate([half, half]).astype(np.float32)[None, :]
    short_in = short_cache.reshape(short_count, slots, 2 * head)
    long_in = long_cache.reshape(long_count, span, 2 * head)
    hbm = pl.BlockSpec(memory_space=pl.ANY)
    vmem = pl.BlockSpec(memory_space=pltpu.VMEM)
    smem = pl.BlockSpec(memory_space=pltpu.SMEM)
    dma = pltpu.SemaphoreType.DMA
    att, part, short_new, long_new = pl.pallas_call(
        attend_kernel,
        name="attend",
        out_shape=(
            jax.ShapeDtypeStruct((short_count, query_width), BF16),
            jax.ShapeDtypeStruct((lrows + 8, head), F32),
            jax.ShapeDtypeStruct(short_in.shape, BF16),
            jax.ShapeDtypeStruct(long_in.shape, BF16),
        ),
        in_specs=[smem, smem, hbm, hbm, vmem, vmem, hbm, hbm, hbm, hbm, hbm],
        out_specs=(vmem, vmem, hbm, hbm),
        scratch_shapes=[
            pltpu.VMEM((short_count, model), BF16),
            pltpu.VMEM((long_count, model), BF16),
            pltpu.VMEM((short_count + 16, model), BF16),
            pltpu.VMEM(w_query.shape, BF16),
            pltpu.VMEM(w_key.shape, BF16),
            pltpu.VMEM(w_value.shape, BF16),
            pltpu.VMEM((total_rows, head), jnp.int32),
            pltpu.VMEM((short_count, query_width), BF16),
            pltpu.VMEM((lrows, head), F32),
            pltpu.VMEM((total_rows, 2 * head), F32),
            pltpu.VMEM(short_in.shape, BF16),
            pltpu.VMEM(long_in.shape, BF16),
            dma((2,)),
            dma((3,)),
            dma((groups,)),
            dma((groups,)),
            dma,
            dma,
        ],
        compiler_params=pltpu.CompilerParams(vmem_limit_bytes=40 * 1024 * 1024),
    )(
        short_lengths,
        long_lengths,
        short_tokens,
        long_tokens,
        norm_gain.reshape(1, model),
        freq,
        w_query,
        w_key,
        w_value,
        short_in,
        long_in,
    )

    chips = tp_size // 2
    grid_size = int(math.isqrt(req_size))
    width = model // tp_size
    hidden, long_hidden = pl.pallas_call(
        functools.partial(project_kernel, tp_size, grid_size),
        name="project",
        out_shape=(
            jax.ShapeDtypeStruct((short_count, model), BF16),
            jax.ShapeDtypeStruct((long_count, model), BF16),
        ),
        in_specs=[vmem, vmem, hbm, hbm, hbm],
        out_specs=(hbm, hbm),
        scratch_shapes=[
            pltpu.VMEM((tp_size, query_width, width), BF16),
            pltpu.VMEM((short_count, width), BF16),
            pltpu.VMEM((long_count, width), BF16),
            pltpu.VMEM((grid_size - 1, lrows + 8, head), F32),
            pltpu.VMEM((grid_size - 1, lrows + 8, head), F32),
            pltpu.VMEM((lrows + 8, head), F32),
            pltpu.VMEM((chips, short_count, width), BF16),
            pltpu.VMEM((chips, short_count, width), BF16),
            pltpu.VMEM((chips, short_count, width), F32),
            pltpu.VMEM((chips - 1, short_count, width), BF16),
            pltpu.VMEM((chips - 1, short_count, width), BF16),
            pltpu.VMEM((tp_size, short_count, width), BF16),
            pltpu.VMEM((tp_size, long_count, width), F32),
            pltpu.VMEM((tp_size - 1, long_count, width), F32),
            pltpu.VMEM((tp_size, long_count, width), BF16),
            dma((tp_size,)),
            dma((2,)),
            dma((grid_size - 1,)),
            dma((grid_size - 1,)),
            dma((grid_size - 1,)),
            dma((grid_size - 1,)),
            dma((chips,)),
            dma((chips,)),
            dma((chips - 1,)),
            dma((chips - 1,)),
            dma((chips - 1,)),
            dma((chips - 1,)),
            dma((chips,)),
            dma((chips,)),
            dma((tp_size - 1,)),
            dma((tp_size - 1,)),
            dma((tp_size - 1,)),
            dma((tp_size - 1,)),
            dma((tp_size,)),
            dma((tp_size,)),
        ],
        compiler_params=pltpu.CompilerParams(
            vmem_limit_bytes=24 * 1024 * 1024, collective_id=0, has_side_effects=True
        ),
    )(att, part, w_out, short_tokens, long_tokens)
    return hidden, long_hidden, short_new.reshape(short_cache.shape), long_new.reshape(long_cache.shape)


def solution(mesh):
    placed = (
        P("req", None),
        P(),
        P(),
        P(None, "tp"),
        P(None, "tp"),
        P(None, "tp"),
        P("tp", None),
        P("req"),
        P(),
        P("req", "tp", None, None),
        P(None, "tp", "req", None),
    )
    return jax.shard_map(
        functools.partial(per_device, mesh.shape["tp"], mesh.shape["req"]),
        mesh=mesh,
        in_specs=placed,
        out_specs=(P("req", None), P(), P("req", "tp", None, None), P(None, "tp", "req", None)),
        check_vma=False,
    )
```
